32 devices in a mesh: dev: 32 (over z, y, x, core).
Axes of the slice: x: 2, y: 2, z: 4, core: 2. Of those that a mesh axis runs over, the one named last changes fastest.
Arguments:
- rhs: float32 [135, 4096], P(None, 'dev')
- diag_blocks: bfloat16 [135, 135, 4096], P(None, None, 'dev')
- precond: bfloat16 [135, 135, 4096], P(None, None, 'dev')
- face_blocks: bfloat16 [6, 45, 45, 4096], P(None, None, None, 'dev'), may hold values from -0.4375 to 0.4375
- nbr_elem: int32 [6, 4096], P(None, 'dev'), may hold values from -1 to 4095, as said below
- nbr_face: int32 [6, 4096], P(None, 'dev'), may hold values from 0 to 5
- live: int32 [32], P('dev'), may hold values from 32 to 128, as said below
Outputs:
- basis: float32 [5, 135, 4096], P(None, None, 'dev')
- hessenberg: float32 [5, 4], replicated
- update: float32 [135, 4096], P(None, 'dev')
The draws below stay inside these ranges and needn't reach their ends.
Inputs may be any that keep to these rules, and one draw needn't show every extreme that they name: `live`: some owner holds 128 elements and some owner holds 32. `nbr_elem`: A non-negative entry names a held element (slot below its owner's live count) whose owner is at most 2 positions away from the face's owner, counted cyclically over the owners; faces of empty slots hold -1. Faces of one owner name elements of any one other owner at most 48 times, and some owner reaches that.
All inputs are finite; a program needn't handle non-finite values.
Results may differ from the reference program's by a relative error of at most 0.025.
Values sent between devices are 32-bit elements; how exact they have to be, the bound alone decides.
A program may use at most 128 MiB of HBM per device.

```python
import jax
import jax.numpy as jnp
import numpy as np
from jax import lax

NV = 5
NP = 135
NF = 45
CAP = 128
STEPS = 4
ELEMS = 4096
HALO_CAP = 48
N_DEV = 32


def dominant(key, lower, upper, reach):
    key_off, key_diag = jax.random.split(key)
    limit = reach / NP ** 0.5
    off_part = jax.random.uniform(key_off, (NP, NP, ELEMS), jnp.float32, -limit, limit)
    diag_part = jax.random.uniform(key_diag, (NP, 1, ELEMS), jnp.float32, lower, upper)
    rows = jnp.arange(NP)[:, None, None]
    cols = jnp.arange(NP)[None, :, None]
    return jnp.where(rows == cols, diag_part, off_part)


def draw_diag_blocks(key, part):
    base = jax.random.fold_in(key, 21)
    blocks = dominant(base, 1.0, 2.0, 0.45)
    return blocks.astype(jnp.bfloat16)


def draw_precond(key, part):
    base = jax.random.fold_in(key, 33)
    blocks = dominant(base, 0.5, 1.0, 0.3)
    return blocks.astype(jnp.bfloat16)


def draw_rhs(key, part):
    key_base, key_rows, key_cols = jax.random.split(jax.random.fold_in(key, 11), 3)
    base = jax.random.normal(key_base, (NP, ELEMS), jnp.float32)
    elem_scale = jnp.exp(jax.random.uniform(key_rows, (1, ELEMS), jnp.float32, jnp.log(0.4), jnp.log(4.0)))
    unk_scale = jnp.exp(jax.random.uniform(key_cols, (NP, 1), jnp.float32, jnp.log(0.4), jnp.log(4.0)))
    return (base * elem_scale * unk_scale).astype(jnp.float32)


def topology(key):
    keys = jax.random.split(jax.random.fold_in(key, 5), 6)
    owners = ELEMS // CAP
    count = CAP * 6
    remote = HALO_CAP
    index = jnp.arange(owners, dtype=jnp.int32)
    live = jax.random.randint(keys[0], (owners,), CAP // 4, CAP + 1, dtype=jnp.int32)
    fullest = jax.random.randint(keys[1], (), 0, owners, dtype=jnp.int32)
    lowest = (fullest + 1 + jax.random.randint(keys[2], (), 0, owners - 1, dtype=jnp.int32)) % owners
    live = jnp.where(index == fullest, CAP, jnp.where(index == lowest, CAP // 4, live)).astype(jnp.int32)
    scores = jax.random.randint(keys[3], (owners, count), 0, 65536, dtype=jnp.int32) * count + jnp.arange(count, dtype=jnp.int32)[None, :]
    order = jnp.argsort(scores, axis=1, stable=True).astype(jnp.int32)
    codes = jnp.where(order < 4 * remote, order // remote, jnp.where(order < count - CAP // 2, 4, 5)).astype(jnp.int32)
    offsets = jnp.array([-2, -1, 1, 2, 0, 0], dtype=jnp.int32)[codes]
    target = (index[:, None] + offsets) % owners
    slot = jax.random.randint(keys[4], (owners, count), 0, live[target], dtype=jnp.int32)
    local_face = jax.random.randint(keys[5], (owners, count), 0, 6, dtype=jnp.int32)
    face_slot = jnp.arange(count, dtype=jnp.int32)[None, :] % CAP
    valid = (face_slot < live[:, None]) & (codes != 5)
    neighbour = jnp.where(valid, target * CAP + slot, -1).astype(jnp.int32).reshape(owners, 6, CAP)
    faces = jnp.where(valid, local_face, 0).astype(jnp.int32).reshape(owners, 6, CAP)
    neighbour = jnp.transpose(neighbour, (1, 0, 2)).reshape(6, ELEMS)
    faces = jnp.transpose(faces, (1, 0, 2)).reshape(6, ELEMS)
    return (live, neighbour, faces)


def draw_live(key, part):
    return topology(key)[0]


def draw_nbr_elem(key, part):
    return topology(key)[1]


def draw_nbr_face(key, part):
    return topology(key)[2]


def block_scale(key, extent, cuts, low, top_value):
    def one(dim, blocks):
        steps = jax.random.uniform(jax.random.fold_in(jax.random.fold_in(key, 6), dim), (blocks,), jnp.float32, low / len(cuts), top_value / len(cuts))
        return jnp.repeat(jnp.exp(steps), extent[dim] // blocks).reshape((-1,) + (1,) * (len(extent) - dim - 1))

    factor_of = one(*cuts[0])
    for cut in cuts[1:]:
        factor_of = factor_of * one(*cut)
    return factor_of


def normal_values(stream_key, extent, spread, most, shards=(), held_as=jnp.bfloat16):
    entries = jax.random.normal(stream_key, extent, jnp.float32) * spread
    if len(shards) > 0:
        entries = block_scale(stream_key, extent, shards, -0.22, 0.18) * entries
    return jnp.clip(entries, min=-most, max=most).astype(held_as)


def setup_inputs(seed: int = 0) -> dict:
    streams_of = jax.random.split(jax.random.key(seed), 8)
    rhs = draw_rhs(jax.random.fold_in(streams_of[7], 71), 0)
    diag_blocks = draw_diag_blocks(jax.random.fold_in(streams_of[7], 71), 0)
    precond = draw_precond(jax.random.fold_in(streams_of[7], 71), 0)
    face_blocks = normal_values(streams_of[3], (6, NF, NF, ELEMS), (4 * NF) ** -0.5, 0.4375, ((3, 32),))
    nbr_elem = draw_nbr_elem(jax.random.fold_in(streams_of[7], 71), 0)
    nbr_face = draw_nbr_face(jax.random.fold_in(streams_of[7], 71), 0)
    live = draw_live(jax.random.fold_in(streams_of[7], 71), 0)
    return {"rhs": rhs, "diag_blocks": diag_blocks, "precond": precond, "face_blocks": face_blocks, "nbr_elem": nbr_elem, "nbr_face": nbr_face, "live": live}


def face_table(variables):
    listing = []
    for face in range(6):
        direction = face // 2
        value = 0 if face % 2 == 0 else 2
        nodes = [node for node in range(27) if (node // 9, node // 3 % 3, node % 3)[direction] == value]
        listing.append([var_index * 27 + node for var_index in range(variables) for node in nodes])
    return np.array(listing, dtype=np.int32)

def owner_slice(array, owner):
    begin = (owner * CAP).astype(jnp.int32)
    return lax.dynamic_slice_in_dim(array, begin, CAP, axis=array.ndim - 1)

def block_apply(blocks, vector):

    def apply_owner(owner):
        block_part = owner_slice(blocks, owner).astype(jnp.float32)
        vector_part = owner_slice(vector, owner).astype(jnp.float32)
        return jnp.einsum('ije,je->ie', block_part, vector_part)
    result = lax.map(apply_owner, jnp.arange(N_DEV, dtype=jnp.int32))
    return jnp.transpose(result, (1, 0, 2)).reshape(NP, ELEMS)

def operate(field, diag_blocks, face_blocks, nbr_elem, nbr_face, table):
    own_part = block_apply(diag_blocks, field)

    def face_owner(owner):
        block_part = owner_slice(face_blocks, owner).astype(jnp.float32)
        vector_part = owner_slice(field, owner).astype(jnp.float32)
        traced = vector_part[table]
        return jnp.einsum('fkme,fme->kfe', block_part, traced)
    contrib = lax.map(face_owner, jnp.arange(N_DEV, dtype=jnp.int32))
    values = jnp.transpose(contrib, (0, 2, 3, 1)).reshape(-1, NF)
    targets = jnp.transpose(nbr_elem.reshape(6, N_DEV, CAP), (1, 0, 2)).reshape(-1)
    faces = jnp.transpose(nbr_face.reshape(6, N_DEV, CAP), (1, 0, 2)).reshape(-1)
    valid = targets >= 0
    safe = jnp.where(valid, targets, 0).astype(jnp.int32)
    values = jnp.where(valid[:, None], values, jnp.zeros_like(values))
    columns = table[faces]
    return own_part.at[columns, safe[:, None]].add(values)

def solve_small(matrix, vector):
    count = matrix.shape[0]
    for column in range(count):
        for row_index in range(column + 1, count):
            factor = matrix[row_index, column] / matrix[column, column]
            matrix = matrix.at[row_index].add(-factor * matrix[column])
            vector = vector.at[row_index].add(-factor * vector[column])
    result = [None] * count
    for row_index in range(count - 1, -1, -1):
        acc = vector[row_index]
        for column in range(row_index + 1, count):
            acc = acc - matrix[row_index, column] * result[column]
        result[row_index] = acc / matrix[row_index, row_index]
    return jnp.stack(result)

def reference(rhs, diag_blocks, precond, face_blocks, nbr_elem, nbr_face, live):
    table = jnp.asarray(face_table(NV))
    slots = jnp.arange(CAP, dtype=jnp.int32)
    live_mask = (slots[None, :] < live[:, None]).reshape(ELEMS).astype(jnp.float32)
    start = rhs * live_mask[None, :]
    scale = 1.0 / float(ELEMS * NP)

    def inner(first, second):
        return jnp.sum(first * second) * scale
    beta = jnp.sqrt(inner(start, start) + 1e-06)
    vectors = [start / beta]
    hessenberg = jnp.zeros((STEPS + 1, STEPS), jnp.float32)
    for step in range(STEPS):
        rounded = vectors[step].astype(jnp.bfloat16)
        applied = block_apply(precond, rounded).astype(jnp.bfloat16)
        image = operate(applied, diag_blocks, face_blocks, nbr_elem, nbr_face, table)
        heights = jnp.stack([inner(vec, image) for vec in vectors])
        rest = image
        for index in range(step + 1):
            rest = rest - heights[index] * vectors[index]
        height = jnp.sqrt(inner(rest, rest) + 1e-06)
        hessenberg = hessenberg.at[:step + 1, step].set(heights)
        hessenberg = hessenberg.at[step + 1, step].set(height)
        vectors.append(rest / height)
    gram = jnp.dot(hessenberg.T, hessenberg, precision=lax.Precision.HIGHEST)
    coeffs = solve_small(gram, beta * hessenberg[0, :])
    combo = vectors[0] * coeffs[0]
    for index in range(1, STEPS):
        combo = combo + coeffs[index] * vectors[index]
    update = block_apply(precond, combo.astype(jnp.bfloat16))
    return (jnp.stack(vectors), hessenberg, update)
```

```python
import functools

import jax
import jax.numpy as jnp
import numpy as np
from jax import lax
from jax.experimental import pallas as pl
from jax.experimental.pallas import tpu as pltpu
from jax.sharding import PartitionSpec as P

STEPS = 4
NODES = 27
FACES = 6
OFFSETS = (1, -1, 2, -2)
MESH = pl.DeviceIdType.MESH


def face_table(variables):
    listing = []
    for face in range(FACES):
        direction = face // 2
        value = 0 if face % 2 == 0 else 2
        nodes = [
            node
            for node in range(NODES)
            if (node // 9, node // 3 % 3, node % 3)[direction] == value
        ]
        listing.append([v * NODES + node for v in range(variables) for node in nodes])
    return np.array(listing, dtype=np.int32)


def spread_table(variables, pitch):
    listing = face_table(variables)
    table = np.zeros((NODES * variables, FACES * pitch), dtype=np.float32)
    for face in range(FACES):
        for entry in range(listing.shape[1]):
            table[listing[face, entry], face * pitch + entry] = 1.0
    return table


def row_sums(block, vector, split):
    half = split // 2
    head = block[:, :half] * vector[None, :half] + block[:, half:split] * vector[None, half:split]
    tail = block[:, split:] * vector[None, split:]
    both = jnp.concatenate([head.astype(jnp.float32), tail.astype(jnp.float32)], axis=1)
    return jnp.sum(both, axis=1)


def kernel(
    owners, live_ref, rhs_ref, nbr_elem_ref, nbr_face_ref, spread_ref, trace_ref,
    diag_hbm, precond_hbm, face_hbm,
    basis_ref, hess_ref, update_ref,
    diag, precond, face, image, fields, contrib, local_place, send_place,
    halo_out, halo_in, dots_out, dots_in,
    load_sems, halo_send, halo_recv, dots_send, dots_recv,
):
    f32, bf16 = jnp.float32, jnp.bfloat16
    unknowns, slots = rhs_ref.shape
    width = face.shape[1]
    pitch = contrib.shape[0]
    lanes = FACES * slots
    me = lax.axis_index("dev")
    scale = 1.0 / float(owners * slots * unknowns)

    loads = [
        pltpu.make_async_copy(src, dst, load_sems.at[k])
        for k, (src, dst) in enumerate(
            [(precond_hbm, precond), (face_hbm, face), (diag_hbm, diag)]
        )
    ]
    for load in loads:
        load.start()

    barrier = pltpu.get_barrier_semaphore()

    def greet(k, carry):
        pl.semaphore_signal(
            barrier, inc=1, device_id=(lax.rem(me + k, owners),), device_id_type=MESH
        )
        return carry

    lax.fori_loop(1, owners, greet, 0)

    live_mask = (lax.broadcasted_iota(jnp.int32, (1, slots), 1) < live_ref[0]).astype(f32)
    start = rhs_ref[...] * live_mask
    on_diag = lax.broadcasted_iota(jnp.int32, (8, 128), 0) == lax.broadcasted_iota(
        jnp.int32, (8, 128), 1
    )

    def begin_total(round_id, rows):
        rows = rows + [jnp.zeros((8 - len(rows), slots), f32)]
        sums = jnp.sum(jnp.concatenate(rows, axis=0), axis=1, keepdims=True)
        mine = jnp.sum(jnp.where(on_diag, sums, 0.0), axis=0, keepdims=True)
        dots_out[round_id] = mine

        def push(k, carry):
            pltpu.make_async_remote_copy(
                src_ref=dots_out.at[round_id],
                dst_ref=dots_in.at[round_id, k - 1],
                send_sem=dots_send.at[round_id],
                recv_sem=dots_recv.at[round_id],
                device_id=(lax.rem(me + k, owners),),
                device_id_type=MESH,
            ).start()
            return carry

        lax.fori_loop(1, owners, push, 0)
        return mine

    def end_total(round_id, mine):
        arrived = dots_in.at[round_id]
        pltpu.make_async_copy(arrived, arrived, dots_recv.at[round_id]).wait()
        return mine + jnp.sum(dots_in[round_id], axis=0)

    first = [jnp.sum(start * start, axis=0, keepdims=True)]
    pl.semaphore_wait(barrier, owners - 1)
    mine = begin_total(0, first)

    goals = nbr_elem_ref[...]
    goal_face = nbr_face_ref[...]
    goal_owner = goals // slots
    goal_slot = goals % slots
    held = goals >= 0
    sub = lax.broadcasted_iota(jnp.int32, (slots, slots), 0)
    lane = lax.broadcasted_iota(jnp.int32, (slots, slots), 1)
    own = held & (goal_owner == me)
    own_slot = jnp.where(own, goal_slot, -1)
    upto = (sub <= lane).astype(bf16)
    every = jnp.ones((slots, slots), bf16)
    keeps = [
        held & (goal_owner == lax.rem(me + offset + owners, owners)) for offset in OFFSETS
    ]
    before = (
        lax.broadcasted_iota(jnp.int32, (FACES, FACES), 1)
        < lax.broadcasted_iota(jnp.int32, (FACES, FACES), 0)
    ).astype(f32)
    for f in range(FACES):
        local_place[:, f * slots : (f + 1) * slots] = (sub == own_slot[f : f + 1]).astype(
            f32
        ).astype(bf16)
    for d, keep in enumerate(keeps):
        mask = keep.astype(f32).astype(bf16)
        within = jnp.dot(mask, upto, preferred_element_type=f32)
        totals = jnp.dot(mask, every, preferred_element_type=f32)
        earlier = jnp.dot(
            before, totals, preferred_element_type=f32, precision=lax.Precision.HIGHEST
        )
        rank = jnp.where(keep, (within + earlier).astype(jnp.int32) - 1, -1)
        for f in range(FACES):
            send_place[d * 128 : (d + 1) * 128, f * slots : (f + 1) * slots] = (
                sub == rank[f : f + 1]
            ).astype(f32).astype(bf16)
    for f in range(FACES):
        at = slice(f * slots, (f + 1) * slots)
        contrib[width : width + 1, at] = goal_slot[f : f + 1].astype(f32)
        contrib[width + 1 : width + 2, at] = goal_face[f : f + 1].astype(f32) + 1.0
        contrib[width + 2 : pitch, at] = jnp.zeros((pitch - width - 2, slots), f32)
    face_row = jnp.concatenate([goal_face[f : f + 1] for f in range(FACES)], axis=1)

    def by_lane(row, index):
        return row[:, index : index + 1]

    norm = by_lane(end_total(0, mine), 0) * scale
    beta = jnp.sqrt(norm + 1e-06)
    basis_ref[0] = start / beta
    cross = {(0, 0): norm / (beta * beta)}
    hess = {}
    arrived_place = None

    for step in range(STEPS):
        rounded = basis_ref[step].astype(bf16)
        if step == 0:
            loads[0].wait()

        def precondition(b, carry):
            at = pl.ds(pl.multiple_of(b * 8, 8), 8)
            fields[step, at, :] = row_sums(precond[at], rounded, 128)
            return carry

        whole = unknowns // 8
        lax.fori_loop(0, whole, precondition, 0)
        fields[step, whole * 8 : unknowns, :] = row_sums(
            precond[whole * 8 : unknowns], rounded, 128
        )
        applied = fields[step, :unknowns, :].astype(bf16)
        traced = jnp.dot(trace_ref[...], applied, preferred_element_type=f32).astype(bf16)
        if step == 0:
            loads[1].wait()
        for f in range(FACES):
            vector = traced[f * pitch : f * pitch + width]
            at = slice(f * slots, (f + 1) * slots)
            for k in range(0, width, 8):
                top = min(k + 8, width)
                contrib[k:top, at] = row_sums(face[f, k:top], vector, 32)
        sent = contrib[...].astype(bf16)
        packed = lax.dot_general(
            sent, send_place[...], (((1,), (1,)), ((), ())), preferred_element_type=f32
        )
        for d in range(len(OFFSETS)):
            halo_out[step, d] = packed[:, d * 128 : (d + 1) * 128]
        copies = []
        for d, offset in enumerate(OFFSETS):
            copies.append(
                pltpu.make_async_remote_copy(
                    src_ref=halo_out.at[step, d],
                    dst_ref=halo_in.at[step, d],
                    send_sem=halo_send.at[step, d],
                    recv_sem=halo_recv.at[step, d],
                    device_id=(lax.rem(me + offset + owners, owners),),
                    device_id_type=MESH,
                )
            )
            copies[-1].start()

        if step == 0:
            loads[2].wait()

        def diagonal(b, carry):
            at = pl.ds(pl.multiple_of(b * 8, 8), 8)
            image[at, :] = row_sums(diag[at], applied, 128)
            return carry

        lax.fori_loop(0, whole, diagonal, 0)
        image[whole * 8 : unknowns, :] = row_sums(diag[whole * 8 : unknowns], applied, 128)

        def deliver(values, faces_at, place, shift):
            placed = jnp.concatenate(
                [jnp.where(faces_at == g + shift, values, 0.0) for g in range(FACES)], axis=0
            ).astype(bf16)
            return lax.dot_general(
                placed, place, (((1,), (1,)), ((), ())), preferred_element_type=f32
            )

        at_faces = deliver(contrib[...], face_row, local_place[...], 0)
        for copy in copies:
            copy.wait_recv()
        got = jnp.concatenate([halo_in[step, d] for d in range(len(OFFSETS))], axis=1)
        got_slot = got[width : width + 1].astype(jnp.int32)
        got_face = got[width + 1 : width + 2].astype(jnp.int32)
        if step == 0:
            spots = lax.broadcasted_iota(jnp.int32, (slots, got.shape[1]), 0)
            arrived_place = (spots == got_slot).astype(f32).astype(bf16)
        at_faces = at_faces + deliver(got, got_face, arrived_place, 1)
        total = image[:unknowns, :] + jnp.dot(
            spread_ref[...], at_faces.astype(bf16), preferred_element_type=f32
        )
        vectors = [basis_ref[i] for i in range(step + 1)]
        mine = begin_total(
            step + 1,
            [jnp.sum(v * total, axis=0, keepdims=True) for v in vectors]
            + [jnp.sum(total * total, axis=0, keepdims=True)],
        )
        summed = end_total(step + 1, mine) * scale
        heights = [by_lane(summed, i) for i in range(step + 1)]
        rest = total
        for h, v in zip(heights, vectors):
            rest = rest - h * v
        along = [
            heights[i]
            - sum(heights[k] * cross[min(i, k), max(i, k)] for k in range(step + 1))
            for i in range(step + 1)
        ]
        square = by_lane(summed, step + 1) - sum(
            heights[i] * (heights[i] + along[i]) for i in range(step + 1)
        )
        square = jnp.maximum(square, 0.0)
        height = jnp.sqrt(square + 1e-06)
        inverse = 1.0 / height
        basis_ref[step + 1] = rest * inverse
        for i in range(step + 1):
            hess[i, step] = heights[i]
            cross[i, step + 1] = along[i] * inverse
        hess[step + 1, step] = height
        cross[step + 1, step + 1] = square * inverse * inverse

    rows = lax.broadcasted_iota(jnp.int32, hess_ref.shape, 0)
    cols = lax.broadcasted_iota(jnp.int32, hess_ref.shape, 1)
    table = jnp.zeros(hess_ref.shape, f32)
    for (i, j), value in hess.items():
        table = jnp.where((rows == i) & (cols == j), value, table)
    hess_ref[...] = table

    matrix = [
        [
            sum(hess[r, i] * hess[r, j] for r in range(min(i, j) + 2))
            for j in range(STEPS)
        ]
        for i in range(STEPS)
    ]
    vector = [beta * hess[0, j] for j in range(STEPS)]
    for c in range(STEPS):
        pivot = 1.0 / matrix[c][c]
        for r in range(c + 1, STEPS):
            factor = matrix[r][c] * pivot
            for k in range(c, STEPS):
                matrix[r][k] = matrix[r][k] - factor * matrix[c][k]
            vector[r] = vector[r] - factor * vector[c]
    coeffs = [None] * STEPS
    for r in range(STEPS - 1, -1, -1):
        acc = vector[r]
        for k in range(r + 1, STEPS):
            acc = acc - matrix[r][k] * coeffs[k]
        coeffs[r] = acc / matrix[r][r]
    update = coeffs[0] * fields[0, :unknowns, :]
    for i in range(1, STEPS):
        update = update + coeffs[i] * fields[i, :unknowns, :]
    update_ref[...] = update

    for step in range(STEPS):
        for d in range(len(OFFSETS)):
            out = halo_out.at[step, d]
            pltpu.make_async_copy(out, out, halo_send.at[step, d]).wait()
    for round_id in range(STEPS + 1):
        arrived = dots_in.at[round_id]
        pltpu.make_async_copy(arrived, arrived, dots_send.at[round_id]).wait()


def per_device(rhs, diag_blocks, precond, face_blocks, nbr_elem, nbr_face, live):
    unknowns, slots = rhs.shape
    width = face_blocks.shape[1]
    owners = lax.axis_size("dev")
    variables = unknowns // NODES
    pitch = (width + 2 + 7) // 8 * 8
    padded = (unknowns + 7) // 8 * 8
    table = spread_table(variables, pitch)
    spread = jnp.asarray(table, jnp.bfloat16)
    trace = jnp.asarray(table.T, jnp.bfloat16)
    f32, bf16 = jnp.float32, jnp.bfloat16
    vmem = pl.BlockSpec(memory_space=pltpu.VMEM)
    smem = pl.BlockSpec(memory_space=pltpu.SMEM)
    hbm = pl.BlockSpec(memory_space=pl.ANY)
    sides = len(OFFSETS)
    dma = pltpu.SemaphoreType.DMA
    return pl.pallas_call(
        functools.partial(kernel, owners),
        out_shape=(
            jax.ShapeDtypeStruct((STEPS + 1, unknowns, slots), f32),
            jax.ShapeDtypeStruct((STEPS + 1, STEPS), f32),
            jax.ShapeDtypeStruct((unknowns, slots), f32),
        ),
        in_specs=[smem, vmem, vmem, vmem, vmem, vmem, hbm, hbm, hbm],
        out_specs=(vmem, vmem, vmem),
        scratch_shapes=[
            pltpu.VMEM(diag_blocks.shape, bf16),
            pltpu.VMEM(precond.shape, bf16),
            pltpu.VMEM(face_blocks.shape, bf16),
            pltpu.VMEM((padded, slots), f32),
            pltpu.VMEM((STEPS, padded, slots), f32),
            pltpu.VMEM((pitch, FACES * slots), f32),
            pltpu.VMEM((slots, FACES * slots), bf16),
            pltpu.VMEM((sides * 128, FACES * slots), bf16),
            pltpu.VMEM((STEPS, sides, pitch, 128), f32),
            pltpu.VMEM((STEPS, sides, pitch, 128), f32),
            pltpu.VMEM((STEPS + 1, 1, 128), f32),
            pltpu.VMEM((STEPS + 1, owners - 1, 1, 128), f32),
            dma((3,)),
            dma((STEPS, sides)),
            dma((STEPS, sides)),
            dma((STEPS + 1,)),
            dma((STEPS + 1,)),
        ],
        compiler_params=pltpu.CompilerParams(
            collective_id=0, has_side_effects=True, vmem_limit_bytes=56 * 1024 * 1024
        ),
    )(live, rhs, nbr_elem, nbr_face, spread, trace, diag_blocks, precond, face_blocks)


def solution(mesh):
    in_specs = (
        P(None, "dev"),
        P(None, None, "dev"),
        P(None, None, "dev"),
        P(None, None, None, "dev"),
        P(None, "dev"),
        P(None, "dev"),
        P("dev"),
    )
    out_specs = (P(None, None, "dev"), P(), P(None, "dev"))
    return jax.shard_map(
        per_device, mesh=mesh, in_specs=in_specs, out_specs=out_specs, check_vma=False
    )
```

```python
import functools

import jax
import jax.numpy as jnp
import numpy as np
from jax import lax
from jax.experimental import pallas as pl
from jax.experimental.pallas import tpu as pltpu
from jax.sharding import PartitionSpec as P

STEPS = 4
NODES = 27
FACES = 6
OFFSETS = (1, -1, 2, -2)
MESH = pl.DeviceIdType.MESH


def face_table(variables):
    listing = []
    for face in range(FACES):
        direction = face // 2
        value = 0 if face % 2 == 0 else 2
        nodes = [
            node
            for node in range(NODES)
            if (node // 9, node // 3 % 3, node % 3)[direction] == value
        ]
        listing.append([v * NODES + node for v in range(variables) for node in nodes])
    return np.array(listing, dtype=np.int32)


def spread_table(variables, pitch):
    listing = face_table(variables)
    table = np.zeros((NODES * variables, FACES * pitch), dtype=np.float32)
    for face in range(FACES):
        for entry in range(listing.shape[1]):
            table[listing[face, entry], face * pitch + entry] = 1.0
    return table


def row_sums(block, vector, split):
    half = split // 2
    head = block[:, :half] * vector[None, :half] + block[:, half:split] * vector[None, half:split]
    tail = block[:, split:] * vector[None, split:]
    both = jnp.concatenate([head.astype(jnp.float32), tail.astype(jnp.float32)], axis=1)
    return jnp.sum(both, axis=1)


def kernel(
    owners, live_ref, rhs_ref, nbr_elem_ref, nbr_face_ref, spread_ref, trace_ref,
    diag_hbm, precond_hbm, face_hbm,
    basis_ref, hess_ref, update_ref,
    diag, precond, face, images, fields, contrib, local_place, send_place,
    halo_out, halo_in, dots_out, dots_in,
    load_sems, halo_send, halo_recv, dots_send, dots_recv,
):
    f32, bf16 = jnp.float32, jnp.bfloat16
    unknowns, slots = rhs_ref.shape
    width = face.shape[1]
    pitch = contrib.shape[0]
    room = slots // 2
    half = pitch // 2
    me = lax.axis_index("dev")
    scale = 1.0 / float(owners * slots * unknowns)

    loads = [
        pltpu.make_async_copy(src, dst, load_sems.at[k])
        for k, (src, dst) in enumerate(
            [(precond_hbm, precond), (face_hbm, face), (diag_hbm, diag)]
        )
    ]
    for load in loads:
        load.start()

    barrier = pltpu.get_barrier_semaphore()

    def greet(k, carry):
        pl.semaphore_signal(
            barrier, inc=1, device_id=(lax.rem(me + k, owners),), device_id_type=MESH
        )
        return carry

    lax.fori_loop(1, owners, greet, 0)

    live_mask = (lax.broadcasted_iota(jnp.int32, (1, slots), 1) < live_ref[0]).astype(f32)
    start = rhs_ref[...] * live_mask
    on_diag = lax.broadcasted_iota(jnp.int32, (8, 128), 0) == lax.broadcasted_iota(
        jnp.int32, (8, 128), 1
    )

    def begin_total(round_id, rows):
        rows = rows + [jnp.zeros((8 - len(rows), slots), f32)]
        sums = jnp.sum(jnp.concatenate(rows, axis=0), axis=1, keepdims=True)
        mine = jnp.sum(jnp.where(on_diag, sums, 0.0), axis=0, keepdims=True)
        dots_out[round_id] = mine

        def push(k, carry):
            pltpu.make_async_remote_copy(
                src_ref=dots_out.at[round_id],
                dst_ref=dots_in.at[round_id, k - 1],
                send_sem=dots_send.at[round_id],
                recv_sem=dots_recv.at[round_id],
                device_id=(lax.rem(me + k, owners),),
                device_id_type=MESH,
            ).start()
            return carry

        lax.fori_loop(1, owners, push, 0)
        return mine

    def end_total(round_id, mine):
        arrived = dots_in.at[round_id]
        pltpu.make_async_copy(arrived, arrived, dots_recv.at[round_id]).wait()
        return mine + jnp.sum(dots_in[round_id], axis=0)

    goals = nbr_elem_ref[...]
    goal_face = nbr_face_ref[...]
    goal_owner = goals // slots
    goal_slot = goals % slots
    held = goals >= 0
    sub = lax.broadcasted_iota(jnp.int32, (slots, slots), 0)
    lane = lax.broadcasted_iota(jnp.int32, (slots, slots), 1)
    own = held & (goal_owner == me)
    own_slot = jnp.where(own, goal_slot, -1)
    upto = (sub <= lane).astype(bf16)
    every = jnp.ones((slots, slots), bf16)
    keeps = [
        held & (goal_owner == lax.rem(me + offset + owners, owners)) for offset in OFFSETS
    ]
    before = (
        lax.broadcasted_iota(jnp.int32, (FACES, FACES), 1)
        < lax.broadcasted_iota(jnp.int32, (FACES, FACES), 0)
    ).astype(f32)
    for f in range(FACES):
        local_place[:, f * slots : (f + 1) * slots] = (sub == own_slot[f : f + 1]).astype(
            f32
        ).astype(bf16)
    for d, keep in enumerate(keeps):
        mask = keep.astype(f32).astype(bf16)
        within = jnp.dot(mask, upto, preferred_element_type=f32)
        totals = jnp.dot(mask, every, preferred_element_type=f32)
        earlier = jnp.dot(
            before, totals, preferred_element_type=f32, precision=lax.Precision.HIGHEST
        )
        rank = jnp.where(keep, (within + earlier).astype(jnp.int32) - 1, -1)
        for f in range(FACES):
            send_place[d * room : (d + 1) * room, f * slots : (f + 1) * slots] = (
                sub[:room] == rank[f : f + 1]
            ).astype(f32).astype(bf16)
    for f in range(FACES):
        at = slice(f * slots, (f + 1) * slots)
        contrib[width : width + 1, at] = goal_slot[f : f + 1].astype(f32)
        contrib[width + 1 : width + 2, at] = goal_face[f : f + 1].astype(f32) + 1.0
        contrib[width + 2 : pitch, at] = jnp.zeros((pitch - width - 2, slots), f32)
    pl.semaphore_wait(barrier, owners - 1)
    face_row = jnp.concatenate([goal_face[f : f + 1] for f in range(FACES)], axis=1)

    def by_lane(row, index):
        return row[:, index : index + 1]

    left = lax.broadcasted_iota(jnp.int32, (half, slots), 1) < room

    def fold(wide):
        top, low = wide[:half], wide[half:]
        return (
            jnp.where(left, top, pltpu.roll(low, room, 1)),
            jnp.where(left, pltpu.roll(top, room, 1), low),
        )

    def unfold(one, two):
        return jnp.concatenate(
            [
                jnp.where(left, one, pltpu.roll(two, room, 1)),
                jnp.where(left, pltpu.roll(one, room, 1), two),
            ],
            axis=0,
        )

    def deliver(values, faces_at, place, shift):
        placed = jnp.concatenate(
            [jnp.where(faces_at == g + shift, values, 0.0) for g in range(FACES)], axis=0
        ).astype(bf16)
        at_faces = lax.dot_general(
            placed, place, (((1,), (1,)), ((), ())), preferred_element_type=f32
        )
        return jnp.dot(spread_ref[...], at_faces.astype(bf16), preferred_element_type=f32)

    cross = {}
    hess = {}
    arrived_place = None
    whole = unknowns // 8
    beta = None
    shift = 1.0

    def normalise(step, mine):
        summed = end_total(step, mine) * scale
        last = step - 1
        heights = [by_lane(summed, i) for i in range(step)]
        rest = images[last, :unknowns, :]
        for i, h in enumerate(heights):
            rest = rest - h * basis_ref[i]
        along = [
            heights[i]
            - sum(heights[k] * cross[min(i, k), max(i, k)] for k in range(step))
            for i in range(step)
        ]
        square = by_lane(summed, step) - sum(
            heights[i] * (heights[i] + along[i]) for i in range(step)
        )
        square = jnp.maximum(square, 0.0)
        height = jnp.sqrt(square + 1e-06)
        inverse = 1.0 / height
        basis_ref[step] = rest * inverse
        for i in range(step):
            hess[i, last] = heights[i]
            cross[i, step] = along[i] * inverse
        hess[step, last] = height
        cross[step, step] = square * inverse * inverse
        return heights, inverse

    for step in range(STEPS):
        if step == 0:
            source = start
        else:
            source = images[step - 1, :unknowns, :] - shift * basis_ref[step - 1]
        rounded = source.astype(bf16)
        if step == 0:
            loads[0].wait()

        def precondition(b, carry):
            at = pl.ds(pl.multiple_of(b * 8, 8), 8)
            fields[step, at, :] = row_sums(precond[at], rounded, 128)
            return carry

        lax.fori_loop(0, whole, precondition, 0)
        fields[step, whole * 8 : unknowns, :] = row_sums(
            precond[whole * 8 : unknowns], rounded, 128
        )
        applied = fields[step, :unknowns, :].astype(bf16)
        traced = jnp.dot(trace_ref[...], applied, preferred_element_type=f32).astype(bf16)
        if step == 0:
            loads[1].wait()
        for f in range(FACES):
            vector = traced[f * pitch : f * pitch + width]
            at = slice(f * slots, (f + 1) * slots)
            for k in range(0, width, 8):
                top = min(k + 8, width)
                contrib[k:top, at] = row_sums(face[f, k:top], vector, 32)
        packed = lax.dot_general(
            contrib[...].astype(bf16),
            send_place[...],
            (((1,), (1,)), ((), ())),
            preferred_element_type=f32,
        )
        for d in range(0, len(OFFSETS), 2):
            halo_out[step, d], halo_out[step, d + 1] = fold(
                packed[:, d * room : (d + 2) * room]
            )
        copies = []
        for d, offset in enumerate(OFFSETS):
            copies.append(
                pltpu.make_async_remote_copy(
                    src_ref=halo_out.at[step, d],
                    dst_ref=halo_in.at[step, d],
                    send_sem=halo_send.at[step, d],
                    recv_sem=halo_recv.at[step, d],
                    device_id=(lax.rem(me + offset + owners, owners),),
                    device_id_type=MESH,
                )
            )
            copies[-1].start()

        if step == 0:
            products = [start * start]
        else:
            newest = images[step - 1, :unknowns, :]
            products = [basis_ref[i] * newest for i in range(step)] + [newest * newest]
        mine = begin_total(step, [jnp.sum(x, axis=0, keepdims=True) for x in products])

        if step == 0:
            loads[2].wait()

        def diagonal(b, carry):
            at = pl.ds(pl.multiple_of(b * 8, 8), 8)
            images[step, at, :] = row_sums(diag[at], applied, 128)
            return carry

        lax.fori_loop(0, whole, diagonal, 0)
        images[step, whole * 8 : unknowns, :] = row_sums(
            diag[whole * 8 : unknowns], applied, 128
        )
        total = images[step, :unknowns, :] + deliver(
            contrib[...], face_row, local_place[...], 0
        )
        for copy in copies:
            copy.wait_recv()
        got = jnp.concatenate(
            [
                unfold(halo_in[step, d], halo_in[step, d + 1])
                for d in range(0, len(OFFSETS), 2)
            ],
            axis=1,
        )
        got_slot = got[width : width + 1].astype(jnp.int32)
        got_face = got[width + 1 : width + 2].astype(jnp.int32)
        if step == 0:
            spots = lax.broadcasted_iota(jnp.int32, (slots, got.shape[1]), 0)
            arrived_place = (spots == got_slot).astype(f32).astype(bf16)
        total = total + deliver(got, got_face, arrived_place, 1)
        if step == 0:
            norm = by_lane(end_total(0, mine), 0) * scale
            beta = jnp.sqrt(norm + 1e-06)
            inverse = 1.0 / beta
            basis_ref[0] = start * inverse
            cross[0, 0] = norm * inverse * inverse
            images[0, :unknowns, :] = total * inverse
            fields[0, :unknowns, :] = fields[0, :unknowns, :] * inverse
        else:
            heights, inverse = normalise(step, mine)
            heights[step - 1] = heights[step - 1] - shift
            field = fields[step, :unknowns, :]
            for i in range(step):
                total = total - heights[i] * images[i, :unknowns, :]
                field = field - heights[i] * fields[i, :unknowns, :]
            images[step, :unknowns, :] = total * inverse
            fields[step, :unknowns, :] = field * inverse
            shift = hess[step - 1, step - 1]

    newest = images[STEPS - 1, :unknowns, :]
    products = [basis_ref[i] * newest for i in range(STEPS)] + [newest * newest]
    normalise(
        STEPS, begin_total(STEPS, [jnp.sum(x, axis=0, keepdims=True) for x in products])
    )

    rows = lax.broadcasted_iota(jnp.int32, hess_ref.shape, 0)
    cols = lax.broadcasted_iota(jnp.int32, hess_ref.shape, 1)
    table = jnp.zeros(hess_ref.shape, f32)
    for (i, j), value in hess.items():
        table = jnp.where((rows == i) & (cols == j), value, table)
    hess_ref[...] = table

    matrix = [
        [
            sum(hess[r, i] * hess[r, j] for r in range(min(i, j) + 2))
            for j in range(STEPS)
        ]
        for i in range(STEPS)
    ]
    vector = [beta * hess[0, j] for j in range(STEPS)]
    for c in range(STEPS):
        pivot = 1.0 / matrix[c][c]
        for r in range(c + 1, STEPS):
            factor = matrix[r][c] * pivot
            for k in range(c, STEPS):
                matrix[r][k] = matrix[r][k] - factor * matrix[c][k]
            vector[r] = vector[r] - factor * vector[c]
    coeffs = [None] * STEPS
    for r in range(STEPS - 1, -1, -1):
        acc = vector[r]
        for k in range(r + 1, STEPS):
            acc = acc - matrix[r][k] * coeffs[k]
        coeffs[r] = acc / matrix[r][r]
    update = coeffs[0] * fields[0, :unknowns, :]
    for i in range(1, STEPS):
        update = update + coeffs[i] * fields[i, :unknowns, :]
    update_ref[...] = update

    for step in range(STEPS):
        for d in range(len(OFFSETS)):
            out = halo_out.at[step, d]
            pltpu.make_async_copy(out, out, halo_send.at[step, d]).wait()
    for round_id in range(STEPS + 1):
        arrived = dots_in.at[round_id]
        pltpu.make_async_copy(arrived, arrived, dots_send.at[round_id]).wait()


def per_device(rhs, diag_blocks, precond, face_blocks, nbr_elem, nbr_face, live):
    unknowns, slots = rhs.shape
    width = face_blocks.shape[1]
    owners = lax.axis_size("dev")
    variables = unknowns // NODES
    pitch = (width + 2 + 15) // 16 * 16
    padded = (unknowns + 7) // 8 * 8
    table = spread_table(variables, pitch)
    spread = jnp.asarray(table, jnp.bfloat16)
    trace = jnp.asarray(table.T, jnp.bfloat16)
    f32, bf16 = jnp.float32, jnp.bfloat16
    vmem = pl.BlockSpec(memory_space=pltpu.VMEM)
    smem = pl.BlockSpec(memory_space=pltpu.SMEM)
    hbm = pl.BlockSpec(memory_space=pl.ANY)
    sides = len(OFFSETS)
    dma = pltpu.SemaphoreType.DMA
    return pl.pallas_call(
        functools.partial(kernel, owners),
        out_shape=(
            jax.ShapeDtypeStruct((STEPS + 1, unknowns, slots), f32),
            jax.ShapeDtypeStruct((STEPS + 1, STEPS), f32),
            jax.ShapeDtypeStruct((unknowns, slots), f32),
        ),
        in_specs=[smem, vmem, vmem, vmem, vmem, vmem, hbm, hbm, hbm],
        out_specs=(vmem, vmem, vmem),
        scratch_shapes=[
            pltpu.VMEM(diag_blocks.shape, bf16),
            pltpu.VMEM(precond.shape, bf16),
            pltpu.VMEM(face_blocks.shape, bf16),
            pltpu.VMEM((STEPS, padded, slots), f32),
            pltpu.VMEM((STEPS, padded, slots), f32),
            pltpu.VMEM((pitch, FACES * slots), f32),
            pltpu.VMEM((slots, FACES * slots), bf16),
            pltpu.VMEM((sides * (slots // 2), FACES * slots), bf16),
            pltpu.VMEM((STEPS, sides, pitch // 2, slots), f32),
            pltpu.VMEM((STEPS, sides, pitch // 2, slots), f32),
            pltpu.VMEM((STEPS + 1, 1, 128), f32),
            pltpu.VMEM((STEPS + 1, owners - 1, 1, 128), f32),
            dma((3,)),
            dma((STEPS, sides)),
            dma((STEPS, sides)),
            dma((STEPS + 1,)),
            dma((STEPS + 1,)),
        ],
        compiler_params=pltpu.CompilerParams(
            collective_id=0, has_side_effects=True, vmem_limit_bytes=56 * 1024 * 1024
        ),
    )(live, rhs, nbr_elem, nbr_face, spread, trace, diag_blocks, precond, face_blocks)


def solution(mesh):
    in_specs = (
        P(None, "dev"),
        P(None, None, "dev"),
        P(None, None, "dev"),
        P(None, None, None, "dev"),
        P(None, "dev"),
        P(None, "dev"),
        P("dev"),
    )
    out_specs = (P(None, None, "dev"), P(), P(None, "dev"))
    return jax.shard_map(
        per_device, mesh=mesh, in_specs=in_specs, out_specs=out_specs, check_vma=False
    )
```

```python
import functools

import jax
import jax.numpy as jnp
import numpy as np
from jax import lax
from jax.experimental import pallas as pl
from jax.experimental.pallas import tpu as pltpu
from jax.sharding import PartitionSpec as P

STEPS = 4
NODES = 27
FACES = 6
OFFSETS = (1, -1, 2, -2)
MESH = pl.DeviceIdType.MESH


def face_table(variables):
    listing = []
    for face in range(FACES):
        direction = face // 2
        value = 0 if face % 2 == 0 else 2
        nodes = [
            node
            for node in range(NODES)
            if (node // 9, node // 3 % 3, node % 3)[direction] == value
        ]
        listing.append([v * NODES + node for v in range(variables) for node in nodes])
    return np.array(listing, dtype=np.int32)


def spread_table(variables, pitch):
    listing = face_table(variables)
    table = np.zeros((NODES * variables, FACES * pitch), dtype=np.float32)
    for face in range(FACES):
        for entry in range(listing.shape[1]):
            table[listing[face, entry], face * pitch + entry] = 1.0
    return table


def row_sums(main, tail, lead, first, count, vector, rest):
    f32 = jnp.float32
    height, double = main.shape[-2:]
    lanes = double // 2
    tiles = height // 8
    sums = []
    for r in range(count):
        at = lead + (first + r,)
        products = [
            main[at + (slice(c * 8, c * 8 + 8),)] * vector[c * 8 : c * 8 + 8]
            for c in range(tiles)
        ]
        pairs = [(products[c] + products[c + 1]).astype(f32) for c in range(0, tiles, 2)]
        parts = [p[:, :lanes] for p in pairs] + [p[:, lanes:] for p in pairs]
        parts.append((tail[at] * rest).astype(f32))
        sums.append(jnp.sum(jnp.concatenate(parts, axis=0), axis=0, keepdims=True))
    return jnp.concatenate(sums, axis=0)


def kernel(
    owners, live_ref, rhs_ref, nbr_elem_ref, nbr_face_ref, spread_ref, trace_ref,
    diag_hbm, precond_hbm, face_hbm,
    basis_ref, hess_ref, update_ref,
    diag, diag_tail, precond, precond_tail, face, face_tail, images, fields, contrib, local_place, send_place,
    halo_out, halo_in, dots_out, dots_in,
    load_sems, halo_send, halo_recv, dots_send, dots_recv,
):
    f32, bf16 = jnp.float32, jnp.bfloat16
    unknowns, slots = rhs_ref.shape
    width = face_hbm.shape[1]
    pitch = contrib.shape[0]
    room = slots // 2
    half = pitch // 2
    me = lax.axis_index("dev")
    scale = 1.0 / float(owners * slots * unknowns)

    loads = []
    for k, (src, main, tail) in enumerate(
        ((precond_hbm, precond, precond_tail), (face_hbm, face, face_tail), (diag_hbm, diag, diag_tail))
    ):
        height, inputs = main.shape[-2], src.shape[-2]
        lead = (slice(None),) * (len(main.shape) - 2)
        pieces = [
            (src.at[lead + (pl.ds(0, height),)], main.at[lead + (slice(None), pl.ds(0, slots))]),
            (
                src.at[lead + (pl.ds(height, height),)],
                main.at[lead + (slice(None), pl.ds(slots, slots))],
            ),
            (src.at[lead + (pl.ds(2 * height, inputs - 2 * height),)], tail),
        ]
        loads.append(
            [
                pltpu.make_async_copy(*piece, load_sems.at[3 * k + m])
                for m, piece in enumerate(pieces)
            ]
        )
        for piece in loads[-1]:
            piece.start()

    def loaded(k):
        for piece in loads[k]:
            piece.wait()

    barrier = pltpu.get_barrier_semaphore()

    def greet(k, carry):
        pl.semaphore_signal(
            barrier, inc=1, device_id=(lax.rem(me + k, owners),), device_id_type=MESH
        )
        return carry

    lax.fori_loop(1, owners, greet, 0)

    live_mask = (lax.broadcasted_iota(jnp.int32, (1, slots), 1) < live_ref[0]).astype(f32)
    start = rhs_ref[...] * live_mask
    on_diag = lax.broadcasted_iota(jnp.int32, (8, 128), 0) == lax.broadcasted_iota(
        jnp.int32, (8, 128), 1
    )

    def begin_total(round_id, rows):
        rows = rows + [jnp.zeros((8 - len(rows), slots), f32)]
        sums = jnp.sum(jnp.concatenate(rows, axis=0), axis=1, keepdims=True)
        mine = jnp.sum(jnp.where(on_diag, sums, 0.0), axis=0, keepdims=True)
        dots_out[round_id] = mine

        def push(k, carry):
            pltpu.make_async_remote_copy(
                src_ref=dots_out.at[round_id],
                dst_ref=dots_in.at[round_id, k - 1],
                send_sem=dots_send.at[round_id],
                recv_sem=dots_recv.at[round_id],
                device_id=(lax.rem(me + k, owners),),
                device_id_type=MESH,
            ).start()
            return carry

        lax.fori_loop(1, owners, push, 0)
        return mine

    def end_total(round_id, mine):
        arrived = dots_in.at[round_id]
        pltpu.make_async_copy(arrived, arrived, dots_recv.at[round_id]).wait()
        return mine + jnp.sum(dots_in[round_id], axis=0)

    goals = nbr_elem_ref[...]
    goal_face = nbr_face_ref[...]
    goal_owner = goals // slots
    goal_slot = goals % slots
    held = goals >= 0
    sub = lax.broadcasted_iota(jnp.int32, (slots, slots), 0)
    lane = lax.broadcasted_iota(jnp.int32, (slots, slots), 1)
    own = held & (goal_owner == me)
    own_slot = jnp.where(own, goal_slot, -1)
    upto = (sub <= lane).astype(bf16)
    every = jnp.ones((slots, slots), bf16)
    keeps = [
        held & (goal_owner == lax.rem(me + offset + owners, owners)) for offset in OFFSETS
    ]
    before = (
        lax.broadcasted_iota(jnp.int32, (FACES, FACES), 1)
        < lax.broadcasted_iota(jnp.int32, (FACES, FACES), 0)
    ).astype(f32)
    for f in range(FACES):
        local_place[:, f * slots : (f + 1) * slots] = (sub == own_slot[f : f + 1]).astype(
            f32
        ).astype(bf16)
    for d, keep in enumerate(keeps):
        mask = keep.astype(f32).astype(bf16)
        within = jnp.dot(mask, upto, preferred_element_type=f32)
        totals = jnp.dot(mask, every, preferred_element_type=f32)
        earlier = jnp.dot(
            before, totals, preferred_element_type=f32, precision=lax.Precision.HIGHEST
        )
        rank = jnp.where(keep, (within + earlier).astype(jnp.int32) - 1, -1)
        for f in range(FACES):
            send_place[d * room : (d + 1) * room, f * slots : (f + 1) * slots] = (
                sub[:room] == rank[f : f + 1]
            ).astype(f32).astype(bf16)
    for f in range(FACES):
        at = slice(f * slots, (f + 1) * slots)
        contrib[width : width + 1, at] = goal_slot[f : f + 1].astype(f32)
        contrib[width + 1 : width + 2, at] = goal_face[f : f + 1].astype(f32) + 1.0
        contrib[width + 2 : pitch, at] = jnp.zeros((pitch - width - 2, slots), f32)
    pl.semaphore_wait(barrier, owners - 1)
    face_row = jnp.concatenate([goal_face[f : f + 1] for f in range(FACES)], axis=1)

    def by_lane(row, index):
        return row[:, index : index + 1]

    left = lax.broadcasted_iota(jnp.int32, (half, slots), 1) < room

    def fold(wide):
        top, low = wide[:half], wide[half:]
        return (
            jnp.where(left, top, pltpu.roll(low, room, 1)),
            jnp.where(left, pltpu.roll(top, room, 1), low),
        )

    def unfold(one, two):
        return jnp.concatenate(
            [
                jnp.where(left, one, pltpu.roll(two, room, 1)),
                jnp.where(left, pltpu.roll(one, room, 1), two),
            ],
            axis=0,
        )

    def deliver(values, faces_at, place, shift):
        placed = jnp.concatenate(
            [jnp.where(faces_at == g + shift, values, 0.0) for g in range(FACES)], axis=0
        ).astype(bf16)
        at_faces = lax.dot_general(
            placed, place, (((1,), (1,)), ((), ())), preferred_element_type=f32
        )
        return jnp.dot(spread_ref[...], at_faces.astype(bf16), preferred_element_type=f32)

    def beside(column, height):
        both = jnp.concatenate([column[:height], column[height : 2 * height]], axis=1)
        return both.astype(bf16), column[2 * height :].astype(bf16)

    cross = {}
    hess = {}
    arrived_place = None
    whole = unknowns // 8
    beta = None
    shift = 1.0

    def normalise(step, mine):
        summed = end_total(step, mine) * scale
        last = step - 1
        heights = [by_lane(summed, i) for i in range(step)]
        rest = images[last, :unknowns, :]
        for i, h in enumerate(heights):
            rest = rest - h * basis_ref[i]
        along = [
            heights[i]
            - sum(heights[k] * cross[min(i, k), max(i, k)] for k in range(step))
            for i in range(step)
        ]
        square = by_lane(summed, step) - sum(
            heights[i] * (heights[i] + along[i]) for i in range(step)
        )
        square = jnp.maximum(square, 0.0)
        height = jnp.sqrt(square + 1e-06)
        inverse = 1.0 / height
        basis_ref[step] = rest * inverse
        for i in range(step):
            hess[i, last] = heights[i]
            cross[i, step] = along[i] * inverse
        hess[step, last] = height
        cross[step, step] = square * inverse * inverse
        return heights, inverse

    for step in range(STEPS):
        if step == 0:
            source = start
        else:
            source = images[step - 1, :unknowns, :] - shift * basis_ref[step - 1]
        rounded, rounded_tail = beside(source, precond.shape[-2])
        if step == 0:
            loaded(0)

        def precondition(b, carry):
            at = pl.ds(pl.multiple_of(b * 8, 8), 8)
            fields[step, at, :] = row_sums(precond, precond_tail, (), b * 8, 8, rounded, rounded_tail)
            return carry

        lax.fori_loop(0, whole, precondition, 0)
        fields[step, whole * 8 : unknowns, :] = row_sums(
            precond, precond_tail, (), whole * 8, unknowns - whole * 8, rounded, rounded_tail
        )
        applied = fields[step, :unknowns, :].astype(bf16)
        halves, halves_tail = beside(fields[step, :unknowns, :], diag.shape[-2])
        traced = jnp.dot(trace_ref[...], applied, preferred_element_type=f32)
        if step == 0:
            loaded(1)
        for f in range(FACES):
            vector, rest = beside(traced[f * pitch : f * pitch + width], face.shape[-2])
            at = slice(f * slots, (f + 1) * slots)
            for k in range(0, width, 8):
                top = min(k + 8, width)
                contrib[k:top, at] = row_sums(
                    face, face_tail, (f,), k, top - k, vector, rest
                )
        packed = lax.dot_general(
            contrib[...].astype(bf16),
            send_place[...],
            (((1,), (1,)), ((), ())),
            preferred_element_type=f32,
        )
        for d in range(0, len(OFFSETS), 2):
            halo_out[step, d], halo_out[step, d + 1] = fold(
                packed[:, d * room : (d + 2) * room]
            )
        copies = []
        for d, offset in enumerate(OFFSETS):
            copies.append(
                pltpu.make_async_remote_copy(
                    src_ref=halo_out.at[step, d],
                    dst_ref=halo_in.at[step, d],
                    send_sem=halo_send.at[step, d],
                    recv_sem=halo_recv.at[step, d],
                    device_id=(lax.rem(me + offset + owners, owners),),
                    device_id_type=MESH,
                )
            )
            copies[-1].start()

        if step == 0:
            products = [start * start]
        else:
            newest = images[step - 1, :unknowns, :]
            products = [basis_ref[i] * newest for i in range(step)] + [newest * newest]
        mine = begin_total(step, [jnp.sum(x, axis=0, keepdims=True) for x in products])

        if step == 0:
            loaded(2)

        def diagonal(b, carry):
            at = pl.ds(pl.multiple_of(b * 8, 8), 8)
            images[step, at, :] = row_sums(diag, diag_tail, (), b * 8, 8, halves, halves_tail)
            return carry

        lax.fori_loop(0, whole, diagonal, 0)
        images[step, whole * 8 : unknowns, :] = row_sums(
            diag, diag_tail, (), whole * 8, unknowns - whole * 8, halves, halves_tail
        )
        total = images[step, :unknowns, :] + deliver(
            contrib[...], face_row, local_place[...], 0
        )
        for copy in copies:
            copy.wait_recv()
        got = jnp.concatenate(
            [
                unfold(halo_in[step, d], halo_in[step, d + 1])
                for d in range(0, len(OFFSETS), 2)
            ],
            axis=1,
        )
        got_slot = got[width : width + 1].astype(jnp.int32)
        got_face = got[width + 1 : width + 2].astype(jnp.int32)
        if step == 0:
            spots = lax.broadcasted_iota(jnp.int32, (slots, got.shape[1]), 0)
            arrived_place = (spots == got_slot).astype(f32).astype(bf16)
        total = total + deliver(got, got_face, arrived_place, 1)
        if step == 0:
            norm = by_lane(end_total(0, mine), 0) * scale
            beta = jnp.sqrt(norm + 1e-06)
            inverse = 1.0 / beta
            basis_ref[0] = start * inverse
            cross[0, 0] = norm * inverse * inverse
            images[0, :unknowns, :] = total * inverse
            fields[0, :unknowns, :] = fields[0, :unknowns, :] * inverse
        else:
            heights, inverse = normalise(step, mine)
            heights[step - 1] = heights[step - 1] - shift
            field = fields[step, :unknowns, :]
            for i in range(step):
                total = total - heights[i] * images[i, :unknowns, :]
                field = field - heights[i] * fields[i, :unknowns, :]
            images[step, :unknowns, :] = total * inverse
            fields[step, :unknowns, :] = field * inverse
            shift = hess[step - 1, step - 1]

    newest = images[STEPS - 1, :unknowns, :]
    products = [basis_ref[i] * newest for i in range(STEPS)] + [newest * newest]
    normalise(
        STEPS, begin_total(STEPS, [jnp.sum(x, axis=0, keepdims=True) for x in products])
    )

    cols = lax.broadcasted_iota(jnp.int32, hess_ref.shape, 0)
    rows = lax.broadcasted_iota(jnp.int32, hess_ref.shape, 1)
    table = jnp.zeros(hess_ref.shape, f32)
    for (i, j), value in hess.items():
        table = jnp.where((rows == i) & (cols == j), value, table)
    hess_ref[...] = table

    matrix = [
        [
            sum(hess[r, i] * hess[r, j] for r in range(min(i, j) + 2))
            for j in range(STEPS)
        ]
        for i in range(STEPS)
    ]
    vector = [beta * hess[0, j] for j in range(STEPS)]
    for c in range(STEPS):
        pivot = 1.0 / matrix[c][c]
        for r in range(c + 1, STEPS):
            factor = matrix[r][c] * pivot
            for k in range(c, STEPS):
                matrix[r][k] = matrix[r][k] - factor * matrix[c][k]
            vector[r] = vector[r] - factor * vector[c]
    coeffs = [None] * STEPS
    for r in range(STEPS - 1, -1, -1):
        acc = vector[r]
        for k in range(r + 1, STEPS):
            acc = acc - matrix[r][k] * coeffs[k]
        coeffs[r] = acc / matrix[r][r]
    update = coeffs[0] * fields[0, :unknowns, :]
    for i in range(1, STEPS):
        update = update + coeffs[i] * fields[i, :unknowns, :]
    update_ref[...] = update

    for step in range(STEPS):
        for d in range(len(OFFSETS)):
            out = halo_out.at[step, d]
            pltpu.make_async_copy(out, out, halo_send.at[step, d]).wait()
    for round_id in range(STEPS + 1):
        arrived = dots_in.at[round_id]
        pltpu.make_async_copy(arrived, arrived, dots_send.at[round_id]).wait()


def per_device(rhs, diag_blocks, precond, face_blocks, nbr_elem, nbr_face, live):
    unknowns, slots = rhs.shape
    width = face_blocks.shape[1]
    owners = lax.axis_size("dev")
    variables = unknowns // NODES
    pitch = (width + 2 + 15) // 16 * 16
    padded = (unknowns + 7) // 8 * 8
    table = spread_table(variables, pitch)
    spread = jnp.asarray(table, jnp.bfloat16)
    trace = jnp.asarray(table.T, jnp.bfloat16)
    f32, bf16 = jnp.float32, jnp.bfloat16
    vmem = pl.BlockSpec(memory_space=pltpu.VMEM)
    smem = pl.BlockSpec(memory_space=pltpu.SMEM)
    hbm = pl.BlockSpec(memory_space=pltpu.HBM)
    sides = len(OFFSETS)
    dma = pltpu.SemaphoreType.DMA

    def halves(block):
        lead, inputs = block.shape[:-2], block.shape[-2]
        split = inputs // 32 * 16
        return [
            pltpu.VMEM(lead + (split, 2 * slots), bf16),
            pltpu.VMEM(lead + (inputs - 2 * split, slots), bf16),
        ]

    basis, hess, update = pl.pallas_call(
        functools.partial(kernel, owners),
        out_shape=(
            jax.ShapeDtypeStruct((STEPS + 1, unknowns, slots), f32),
            jax.ShapeDtypeStruct((STEPS, STEPS + 1), f32),
            jax.ShapeDtypeStruct((unknowns, slots), f32),
        ),
        in_specs=[smem, vmem, vmem, vmem, vmem, vmem, hbm, hbm, hbm],
        out_specs=(vmem, vmem, vmem),
        scratch_shapes=[
            *halves(diag_blocks),
            *halves(precond),
            *halves(face_blocks),
            pltpu.VMEM((STEPS, padded, slots), f32),
            pltpu.VMEM((STEPS, padded, slots), f32),
            pltpu.VMEM((pitch, FACES * slots), f32),
            pltpu.VMEM((slots, FACES * slots), bf16),
            pltpu.VMEM((sides * (slots // 2), FACES * slots), bf16),
            pltpu.VMEM((STEPS, sides, pitch // 2, slots), f32),
            pltpu.VMEM((STEPS, sides, pitch // 2, slots), f32),
            pltpu.VMEM((STEPS + 1, 1, 128), f32),
            pltpu.VMEM((STEPS + 1, owners - 1, 1, 128), f32),
            dma((9,)),
            dma((STEPS, sides)),
            dma((STEPS, sides)),
            dma((STEPS + 1,)),
            dma((STEPS + 1,)),
        ],
        compiler_params=pltpu.CompilerParams(
            collective_id=0, has_side_effects=True, vmem_limit_bytes=52 * 1024 * 1024
        ),
    )(live, rhs, nbr_elem, nbr_face, spread, trace, diag_blocks, precond, face_blocks)
    return basis, hess.T, update


def solution(mesh):
    in_specs = (
        P(None, "dev"),
        P(None, None, "dev"),
        P(None, None, "dev"),
        P(None, None, None, "dev"),
        P(None, "dev"),
        P(None, "dev"),
        P("dev"),
    )
    out_specs = (P(None, None, "dev"), P(), P(None, "dev"))
    return jax.shard_map(
        per_device, mesh=mesh, in_specs=in_specs, out_specs=out_specs, check_vma=False
    )
```

```python
import functools

import jax
import jax.numpy as jnp
import numpy as np
from jax import lax
from jax.experimental import pallas as pl
from jax.experimental.pallas import tpu as pltpu
from jax.sharding import PartitionSpec as P

STEPS = 4
NODES = 27
FACES = 6
OFFSETS = (1, -1, 2, -2)
MESH = pl.DeviceIdType.MESH


def face_table(variables):
    listing = []
    for face in range(FACES):
        direction = face // 2
        value = 0 if face % 2 == 0 else 2
        nodes = [
            node
            for node in range(NODES)
            if (node // 9, node // 3 % 3, node % 3)[direction] == value
        ]
        listing.append([v * NODES + node for v in range(variables) for node in nodes])
    return np.array(listing, dtype=np.int32)


def spread_table(variables, pitch):
    listing = face_table(variables)
    table = np.zeros((NODES * variables, FACES * pitch), dtype=np.float32)
    for face in range(FACES):
        for entry in range(listing.shape[1]):
            table[listing[face, entry], face * pitch + entry] = 1.0
    return table


def row_sums(main, tail, lead, first, count, vector, rest):
    f32 = jnp.float32
    height, double = main.shape[-2:]
    lanes = double // 2
    tiles = height // 8
    sums = []
    for r in range(count):
        at = lead + (first + r,)
        products = [
            main[at + (slice(c * 8, c * 8 + 8),)] * vector[c * 8 : c * 8 + 8]
            for c in range(tiles)
        ]
        pairs = [(products[c] + products[c + 1]).astype(f32) for c in range(0, tiles, 2)]
        parts = [p[:, :lanes] for p in pairs] + [p[:, lanes:] for p in pairs]
        parts.append((tail[at] * rest).astype(f32))
        sums.append(jnp.sum(jnp.concatenate(parts, axis=0), axis=0, keepdims=True))
    return jnp.concatenate(sums, axis=0)


def kernel(
    owners, live_ref, rhs_ref, nbr_elem_ref, nbr_face_ref, spread_ref, trace_ref,
    diag_hbm, precond_hbm, face_hbm,
    basis_ref, hess_ref, update_ref,
    diag, diag_tail, precond, precond_tail, face, face_tail, images, fields, contrib, local_place, send_place,
    halo_out, halo_in, dots_out, dots_in,
    load_sems, halo_send, halo_recv, dots_send, dots_recv,
):
    f32, bf16 = jnp.float32, jnp.bfloat16
    unknowns, slots = rhs_ref.shape
    width = face_hbm.shape[1]
    pitch = contrib.shape[0]
    room = slots // 2
    half = pitch // 2
    me = lax.axis_index("dev")
    scale = 1.0 / float(owners * slots * unknowns)

    loads = []
    for k, (src, main, tail) in enumerate(
        ((precond_hbm, precond, precond_tail), (face_hbm, face, face_tail), (diag_hbm, diag, diag_tail))
    ):
        height, inputs = main.shape[-2], src.shape[-2]
        lead = (slice(None),) * (len(main.shape) - 2)
        pieces = [
            (src.at[lead + (pl.ds(0, height),)], main.at[lead + (slice(None), pl.ds(0, slots))]),
            (
                src.at[lead + (pl.ds(height, height),)],
                main.at[lead + (slice(None), pl.ds(slots, slots))],
            ),
            (src.at[lead + (pl.ds(2 * height, inputs - 2 * height),)], tail),
        ]
        loads.append(
            [
                pltpu.make_async_copy(*piece, load_sems.at[3 * k + m])
                for m, piece in enumerate(pieces)
            ]
        )
        for piece in loads[-1]:
            piece.start()

    def loaded(k):
        for piece in loads[k]:
            piece.wait()

    barrier = pltpu.get_barrier_semaphore()

    def greet(k, carry):
        pl.semaphore_signal(
            barrier, inc=1, device_id=(lax.rem(me + k, owners),), device_id_type=MESH
        )
        return carry

    lax.fori_loop(1, owners, greet, 0)

    live_mask = (lax.broadcasted_iota(jnp.int32, (1, slots), 1) < live_ref[0]).astype(f32)
    start = rhs_ref[...] * live_mask
    on_diag = lax.broadcasted_iota(jnp.int32, (8, 128), 0) == lax.broadcasted_iota(
        jnp.int32, (8, 128), 1
    )

    def begin_total(round_id, rows):
        rows = rows + [jnp.zeros((8 - len(rows), slots), f32)]
        sums = jnp.sum(jnp.concatenate(rows, axis=0), axis=1, keepdims=True)
        mine = jnp.sum(jnp.where(on_diag, sums, 0.0), axis=0, keepdims=True)
        dots_out[round_id] = mine

        def push(k, carry):
            pltpu.make_async_remote_copy(
                src_ref=dots_out.at[round_id],
                dst_ref=dots_in.at[round_id, k - 1],
                send_sem=dots_send.at[round_id],
                recv_sem=dots_recv.at[round_id],
                device_id=(lax.rem(me + k, owners),),
                device_id_type=MESH,
            ).start()
            return carry

        lax.fori_loop(1, owners, push, 0)
        return mine

    def end_total(round_id, mine):
        arrived = dots_in.at[round_id]
        pltpu.make_async_copy(arrived, arrived, dots_recv.at[round_id]).wait()
        return mine + jnp.sum(dots_in[round_id], axis=0)

    goals = nbr_elem_ref[...]
    goal_face = nbr_face_ref[...]
    goal_owner = goals // slots
    goal_slot = goals % slots
    held = goals >= 0
    sub = lax.broadcasted_iota(jnp.int32, (slots, slots), 0)
    lane = lax.broadcasted_iota(jnp.int32, (slots, slots), 1)
    own = held & (goal_owner == me)
    own_slot = jnp.where(own, goal_slot, -1)
    upto = (sub <= lane).astype(bf16)
    every = jnp.ones((slots, slots), bf16)
    keeps = [
        held & (goal_owner == lax.rem(me + offset + owners, owners)) for offset in OFFSETS
    ]
    before = (
        lax.broadcasted_iota(jnp.int32, (FACES, FACES), 1)
        < lax.broadcasted_iota(jnp.int32, (FACES, FACES), 0)
    ).astype(f32)
    for f in range(FACES):
        local_place[:, f * slots : (f + 1) * slots] = (sub == own_slot[f : f + 1]).astype(
            f32
        ).astype(bf16)
    for d, keep in enumerate(keeps):
        mask = keep.astype(f32).astype(bf16)
        within = jnp.dot(mask, upto, preferred_element_type=f32)
        totals = jnp.dot(mask, every, preferred_element_type=f32)
        earlier = jnp.dot(
            before, totals, preferred_element_type=f32, precision=lax.Precision.HIGHEST
        )
        rank = jnp.where(keep, (within + earlier).astype(jnp.int32) - 1, -1)
        for f in range(FACES):
            send_place[d * room : (d + 1) * room, f * slots : (f + 1) * slots] = (
                sub[:room] == rank[f : f + 1]
            ).astype(f32).astype(bf16)
    for f in range(FACES):
        at = slice(f * slots, (f + 1) * slots)
        contrib[width : width + 1, at] = goal_slot[f : f + 1].astype(f32)
        contrib[width + 1 : width + 2, at] = goal_face[f : f + 1].astype(f32) + 1.0
        contrib[width + 2 : pitch, at] = jnp.zeros((pitch - width - 2, slots), f32)
    pl.semaphore_wait(barrier, owners - 1)
    face_row = jnp.concatenate([goal_face[f : f + 1] for f in range(FACES)], axis=1)

    def by_lane(row, index):
        return row[:, index : index + 1]

    left = lax.broadcasted_iota(jnp.int32, (half, slots), 1) < room

    def fold(wide):
        top, low = wide[:half], wide[half:]
        return (
            jnp.where(left, top, pltpu.roll(low, room, 1)),
            jnp.where(left, pltpu.roll(top, room, 1), low),
        )

    def unfold(one, two):
        return jnp.concatenate(
            [
                jnp.where(left, one, pltpu.roll(two, room, 1)),
                jnp.where(left, pltpu.roll(one, room, 1), two),
            ],
            axis=0,
        )

    def deliver(values, faces_at, place, shift):
        placed = jnp.concatenate(
            [jnp.where(faces_at == g + shift, values, 0.0) for g in range(FACES)], axis=0
        ).astype(bf16)
        at_faces = lax.dot_general(
            placed, place, (((1,), (1,)), ((), ())), preferred_element_type=f32
        )
        return jnp.dot(spread_ref[...], at_faces.astype(bf16), preferred_element_type=f32)

    def beside(column, height):
        both = jnp.concatenate([column[:height], column[height : 2 * height]], axis=1)
        return both.astype(bf16), column[2 * height :].astype(bf16)

    cross = {}
    hess = {}
    arrived_place = None
    whole = unknowns // 8
    beta = None
    shift = 1.0

    def normalise(step, mine):
        summed = end_total(step, mine) * scale
        last = step - 1
        heights = [by_lane(summed, i) for i in range(step)]
        rest = images[last, :unknowns, :]
        for i, h in enumerate(heights):
            rest = rest - h * basis_ref[i]
        along = [
            heights[i]
            - sum(heights[k] * cross[min(i, k), max(i, k)] for k in range(step))
            for i in range(step)
        ]
        square = by_lane(summed, step) - sum(
            heights[i] * (heights[i] + along[i]) for i in range(step)
        )
        square = jnp.maximum(square, 0.0)
        height = jnp.sqrt(square + 1e-06)
        inverse = 1.0 / height
        basis_ref[step] = rest * inverse
        for i in range(step):
            hess[i, last] = heights[i]
            cross[i, step] = along[i] * inverse
        hess[step, last] = height
        cross[step, step] = square * inverse * inverse
        return heights, inverse

    for step in range(STEPS):
        if step == 0:
            source = start
        else:
            source = images[step - 1, :unknowns, :] - shift * basis_ref[step - 1]
        rounded, rounded_tail = beside(source, precond.shape[-2])
        if step == 0:
            loaded(0)

        def precondition(b, carry):
            at = pl.ds(pl.multiple_of(b * 8, 8), 8)
            fields[step, at, :] = row_sums(precond, precond_tail, (), b * 8, 8, rounded, rounded_tail)
            return carry

        lax.fori_loop(0, whole, precondition, 0)
        fields[step, whole * 8 : unknowns, :] = row_sums(
            precond, precond_tail, (), whole * 8, unknowns - whole * 8, rounded, rounded_tail
        )
        applied = fields[step, :unknowns, :].astype(bf16)
        halves, halves_tail = beside(fields[step, :unknowns, :], diag.shape[-2])
        traced = jnp.dot(trace_ref[...], applied, preferred_element_type=f32)
        if step == 0:
            loaded(1)
        for f in range(FACES):
            vector, rest = beside(traced[f * pitch : f * pitch + width], face.shape[-2])
            at = slice(f * slots, (f + 1) * slots)
            for k in range(0, width, 8):
                top = min(k + 8, width)
                contrib[k:top, at] = row_sums(
                    face, face_tail, (f,), k, top - k, vector, rest
                )
        packed = lax.dot_general(
            contrib[...].astype(bf16),
            send_place[...],
            (((1,), (1,)), ((), ())),
            preferred_element_type=f32,
        )
        for d in range(0, len(OFFSETS), 2):
            halo_out[step, d], halo_out[step, d + 1] = fold(
                packed[:, d * room : (d + 2) * room]
            )
        copies = []
        for d, offset in enumerate(OFFSETS):
            copies.append(
                pltpu.make_async_remote_copy(
                    src_ref=halo_out.at[step, d],
                    dst_ref=halo_in.at[step, d],
                    send_sem=halo_send.at[step, d],
                    recv_sem=halo_recv.at[step, d],
                    device_id=(lax.rem(me + offset + owners, owners),),
                    device_id_type=MESH,
                )
            )
            copies[-1].start()

        if step == 0:
            products = [start * start]
        else:
            newest = images[step - 1, :unknowns, :]
            products = [basis_ref[i] * newest for i in range(step)] + [newest * newest]
        mine = begin_total(step, [jnp.sum(x, axis=0, keepdims=True) for x in products])

        if step == 0:
            loaded(2)

        def diagonal(b, carry):
            at = pl.ds(pl.multiple_of(b * 8, 8), 8)
            images[step, at, :] = row_sums(diag, diag_tail, (), b * 8, 8, halves, halves_tail)
            return carry

        lax.fori_loop(0, whole, diagonal, 0)
        images[step, whole * 8 : unknowns, :] = row_sums(
            diag, diag_tail, (), whole * 8, unknowns - whole * 8, halves, halves_tail
        )
        total = images[step, :unknowns, :] + deliver(
            contrib[...], face_row, local_place[...], 0
        )
        for copy in copies:
            copy.wait_recv()
        got = jnp.concatenate(
            [
                unfold(halo_in[step, d], halo_in[step, d + 1])
                for d in range(0, len(OFFSETS), 2)
            ],
            axis=1,
        )
        got_slot = got[width : width + 1].astype(jnp.int32)
        got_face = got[width + 1 : width + 2].astype(jnp.int32)
        if step == 0:
            spots = lax.broadcasted_iota(jnp.int32, (slots, got.shape[1]), 0)
            arrived_place = (spots == got_slot).astype(f32).astype(bf16)
        total = total + deliver(got, got_face, arrived_place, 1)
        if step == 0:
            norm = by_lane(end_total(0, mine), 0) * scale
            beta = jnp.sqrt(norm + 1e-06)
            inverse = 1.0 / beta
            basis_ref[0] = start * inverse
            cross[0, 0] = norm * inverse * inverse
            images[0, :unknowns, :] = total * inverse
            fields[0, :unknowns, :] = fields[0, :unknowns, :] * inverse
        else:
            heights, inverse = normalise(step, mine)
            heights[step - 1] = heights[step - 1] - shift
            field = fields[step, :unknowns, :]
            for i in range(step):
                total = total - heights[i] * images[i, :unknowns, :]
                field = field - heights[i] * fields[i, :unknowns, :]
            images[step, :unknowns, :] = total * inverse
            fields[step, :unknowns, :] = field * inverse
            shift = hess[step - 1, step - 1]

    newest = images[STEPS - 1, :unknowns, :]
    products = [basis_ref[i] * newest for i in range(STEPS)] + [newest * newest]
    normalise(
        STEPS, begin_total(STEPS, [jnp.sum(x, axis=0, keepdims=True) for x in products])
    )

    cols = lax.broadcasted_iota(jnp.int32, hess_ref.shape, 0)
    rows = lax.broadcasted_iota(jnp.int32, hess_ref.shape, 1)
    table = jnp.zeros(hess_ref.shape, f32)
    for (i, j), value in hess.items():
        table = jnp.where((rows == i) & (cols == j), value, table)
    hess_ref[...] = table

    matrix = [
        [
            sum(hess[r, i] * hess[r, j] for r in range(min(i, j) + 2))
            for j in range(STEPS)
        ]
        for i in range(STEPS)
    ]
    vector = [beta * hess[0, j] for j in range(STEPS)]
    for c in range(STEPS):
        pivot = 1.0 / matrix[c][c]
        for r in range(c + 1, STEPS):
            factor = matrix[r][c] * pivot
            for k in range(c, STEPS):
                matrix[r][k] = matrix[r][k] - factor * matrix[c][k]
            vector[r] = vector[r] - factor * vector[c]
    coeffs = [None] * STEPS
    for r in range(STEPS - 1, -1, -1):
        acc = vector[r]
        for k in range(r + 1, STEPS):
            acc = acc - matrix[r][k] * coeffs[k]
        coeffs[r] = acc / matrix[r][r]
    update = coeffs[0] * fields[0, :unknowns, :]
    for i in range(1, STEPS):
        update = update + coeffs[i] * fields[i, :unknowns, :]
    update_ref[...] = update

    for step in range(STEPS):
        for d in range(len(OFFSETS)):
            out = halo_out.at[step, d]
            pltpu.make_async_copy(out, out, halo_send.at[step, d]).wait()
    for round_id in range(STEPS + 1):
        arrived = dots_in.at[round_id]
        pltpu.make_async_copy(arrived, arrived, dots_send.at[round_id]).wait()


def hand_over(*refs):
    half = len(refs) // 2
    for source, target in zip(refs[:half], refs[half:]):
        target[...] = source[...]


def per_device(rhs, diag_blocks, precond, face_blocks, nbr_elem, nbr_face, live):
    unknowns, slots = rhs.shape
    width = face_blocks.shape[1]
    owners = lax.axis_size("dev")
    variables = unknowns // NODES
    pitch = (width + 2 + 15) // 16 * 16
    padded = (unknowns + 7) // 8 * 8
    table = spread_table(variables, pitch)
    spread = jnp.asarray(table, jnp.bfloat16)
    trace = jnp.asarray(table.T, jnp.bfloat16)
    f32, bf16 = jnp.float32, jnp.bfloat16
    vmem = pl.BlockSpec(memory_space=pltpu.VMEM)
    smem = pl.BlockSpec(memory_space=pltpu.SMEM)
    hbm = pl.BlockSpec(memory_space=pltpu.HBM)
    sides = len(OFFSETS)
    dma = pltpu.SemaphoreType.DMA

    def halves(block):
        lead, inputs = block.shape[:-2], block.shape[-2]
        split = inputs // 32 * 16
        return [
            pltpu.VMEM(lead + (split, 2 * slots), bf16),
            pltpu.VMEM(lead + (inputs - 2 * split, slots), bf16),
        ]

    basis, hess, update = pl.pallas_call(
        functools.partial(kernel, owners),
        out_shape=(
            jax.ShapeDtypeStruct((STEPS + 1, unknowns, slots), f32),
            jax.ShapeDtypeStruct((STEPS, STEPS + 1), f32),
            jax.ShapeDtypeStruct((unknowns, slots), f32),
        ),
        in_specs=[smem, vmem, vmem, vmem, vmem, vmem, hbm, hbm, hbm],
        out_specs=(vmem, vmem, vmem),
        scratch_shapes=[
            *halves(diag_blocks),
            *halves(precond),
            *halves(face_blocks),
            pltpu.VMEM((STEPS, padded, slots), f32),
            pltpu.VMEM((STEPS, padded, slots), f32),
            pltpu.VMEM((pitch, FACES * slots), f32),
            pltpu.VMEM((slots, FACES * slots), bf16),
            pltpu.VMEM((sides * (slots // 2), FACES * slots), bf16),
            pltpu.VMEM((STEPS, sides, pitch // 2, slots), f32),
            pltpu.VMEM((STEPS, sides, pitch // 2, slots), f32),
            pltpu.VMEM((STEPS + 1, 1, 128), f32),
            pltpu.VMEM((STEPS + 1, owners - 1, 1, 128), f32),
            dma((9,)),
            dma((STEPS, sides)),
            dma((STEPS, sides)),
            dma((STEPS + 1,)),
            dma((STEPS + 1,)),
        ],
        compiler_params=pltpu.CompilerParams(
            collective_id=0, has_side_effects=True, vmem_limit_bytes=60 * 1024 * 1024
        ),
    )(live, rhs, nbr_elem, nbr_face, spread, trace, diag_blocks, precond, face_blocks)
    results = (basis, hess, update)
    basis, hess, update = pl.pallas_call(
        hand_over,
        out_shape=[jax.ShapeDtypeStruct(r.shape, r.dtype) for r in results],
        in_specs=[vmem] * 3,
        out_specs=[vmem] * 3,
    )(*results)
    return basis, hess.T, update


def solution(mesh):
    in_specs = (
        P(None, "dev"),
        P(None, None, "dev"),
        P(None, None, "dev"),
        P(None, None, None, "dev"),
        P(None, "dev"),
        P(None, "dev"),
        P("dev"),
    )
    out_specs = (P(None, None, "dev"), P(), P(None, "dev"))
    return jax.shard_map(
        per_device, mesh=mesh, in_specs=in_specs, out_specs=out_specs, check_vma=False
    )
```
